32 devices in a mesh: seq: 2 (over x), fsdp: 16 (over z, y, core).
Axes of the slice: x: 2, y: 2, z: 4, core: 2. Of those that a mesh axis runs over, the one named last changes fastest.
Arguments:
- layer_input: bfloat16 [16, 1024, 768], P('fsdp', 'seq'), may hold values from -6 to 6
- segment_ids: int32 [16, 1024], P('fsdp'), may hold values from 0 to 5, never falling along the last dimension, each value on 1 to 256 neighbouring positions
- key_valid: int32 [16, 1024], P('fsdp'), may hold values 0 or 1
- first_gain: bfloat16 [2, 768], P(None, 'fsdp'), may hold values from 0.25 to 1.75
- first_shift: bfloat16 [2, 768], P(None, 'fsdp'), may hold values from -1.75 to 1.75
- input_weight: bfloat16 [2, 768, 2304], P(None, 'fsdp'), may hold values from -0.21875 to 0.21875
- query_bias: bfloat16 [2, 768], P(None, 'fsdp'), may hold values from -3 to 3
- value_bias: bfloat16 [2, 768], P(None, 'fsdp'), may hold values from -3 to 3
- output_weight: bfloat16 [2, 768, 768], P(None, 'fsdp'), may hold values from -1.25 to 1.25
- output_bias: bfloat16 [2, 768], P(None, 'fsdp'), may hold values from -1.75 to 1.75
- second_gain: bfloat16 [2, 768], P(None, 'fsdp'), may hold values from 0.25 to 1.75
- second_shift: bfloat16 [2, 768], P(None, 'fsdp'), may hold values from -1.75 to 1.75
- up_weight: bfloat16 [2, 768, 3072], P(None, 'fsdp'), may hold values from -0.21875 to 0.21875
- up_bias: bfloat16 [2, 3072], P(None, 'fsdp'), may hold values from -3 to 3
- down_weight: bfloat16 [2, 3072, 768], P(None, 'fsdp'), may hold values from -0.109375 to 0.109375
- down_bias: bfloat16 [2, 768], P(None, 'fsdp'), may hold values from -1.75 to 1.75
- output_cotangent: bfloat16 [16, 1024, 768], P('fsdp', 'seq'), may hold values from -6 to 6
Outputs:
- layer_output: bfloat16 [16, 1024, 768], P('fsdp', 'seq')
- input_grad: float32 [16, 1024, 768], P('fsdp', 'seq')
- grad_first_gain: float32 [2, 768], P(None, 'fsdp')
- grad_first_shift: float32 [2, 768], P(None, 'fsdp')
- grad_input_weight: float32 [2, 768, 2304], P(None, 'fsdp')
- grad_query_bias: float32 [2, 768], P(None, 'fsdp')
- grad_value_bias: float32 [2, 768], P(None, 'fsdp')
- grad_output_weight: float32 [2, 768, 768], P(None, 'fsdp')
- grad_output_bias: float32 [2, 768], P(None, 'fsdp')
- grad_second_gain: float32 [2, 768], P(None, 'fsdp')
- grad_second_shift: float32 [2, 768], P(None, 'fsdp')
- grad_up_weight: float32 [2, 768, 3072], P(None, 'fsdp')
- grad_up_bias: float32 [2, 3072], P(None, 'fsdp')
- grad_down_weight: float32 [2, 3072, 768], P(None, 'fsdp')
- grad_down_bias: float32 [2, 768], P(None, 'fsdp')
The draws below stay inside these ranges and needn't reach their ends.
Inputs may be any that keep to these rules, and one draw needn't show every extreme that they name: `segment_ids`: along each packed row the ids never fall; each image holds 1 to 256 tokens and one holds exactly 256.
All inputs are finite; a program needn't handle non-finite values. No bound on the sum of `key_valid` on one device may be relied on, other than what follows from the above.
Results may differ from the reference program's by a relative error of at most 0.015.
Values may be sent and summed in bfloat16 or wider, within the bound.
No kernel may reach another device: no remote copies, remote signals or barrier semaphores. Data moves between devices by JAX's collectives and lax.ppermute only.
A program may use at most 256 MiB of HBM per device.

```python
import math
import jax
import jax.numpy as jnp
import numpy as np
from jax import lax

D = 768
H = 12
HD = 64
FF = 3072
L = 1024
LAYERS = 2
SEGS = 6
SEG_MOST = 256
ROWS = 16


def plant(array, own_key, smallest, top_value):
    dims = array.shape
    spot = [jax.random.randint(jax.random.fold_in(own_key, axis), (), 0, dims[axis]) for axis in range(len(dims))]
    array = array.at[tuple(spot)].set(smallest)
    longest = dims.index(max(dims))
    spot[longest] = (spot[longest] + 1) % dims[longest]
    return array.at[tuple(spot)].set(top_value)


def strengthened(values, stream_key, source, target, parts, factor):
    owner, partner = [(jnp.arange(values.shape[position]) // (values.shape[position] // parts)).reshape([-1 if axis == position else 1 for axis in range(values.ndim)]) for position in (source, target)]
    chosen = jax.random.permutation(stream_key, parts)[partner]
    strong = (owner == chosen) | (owner == (partner + parts // 2) % parts)
    return jnp.where(strong, factor * values, values)


def steps_of(stream_key, dims, cuts, smallest, high):
    level, own = 1.0, jax.random.fold_in(stream_key, 6)
    for axis_at, shards_of in cuts:
        draws = jnp.exp(jax.random.uniform(jax.random.fold_in(own, axis_at), (shards_of,), jnp.float32, smallest / len(cuts), high / len(cuts)))
        level = level * jnp.repeat(draws, dims[axis_at] // shards_of).reshape([-1 if axis == axis_at else 1 for axis in range(len(dims))])
    return level


def length_profile(amount, total, reach, slope):
    portions = [(1 << 20) // math.isqrt(rank ** slope) + 1 for rank in range(2, amount + 1)]
    surplus, holding = total - reach - (amount - 1), [1] * (amount - 1)
    while surplus > 0:
        candidates = [i for i in range(amount - 1) if holding[i] < reach]
        pool, budget = sum([portions[i] for i in candidates]), surplus
        for i in candidates:
            addition = min(reach - holding[i], max(1, budget * portions[i] // pool), surplus)
            holding[i] = holding[i] + addition
            surplus = surplus - addition
    return np.array([reach] + holding)


def uneven_parts(stream_key, number_of, total, most, slope):
    if number_of == 2:
        one = jax.random.randint(stream_key, (), max(1, total - most), min(most, total - 1) + 1)
        return jnp.stack([one, total - one])
    lengths = jnp.asarray(length_profile(number_of, total, most, slope), jnp.int32)
    twos = (number_of - 1) // 2
    donor, sink = lengths[1:1 + 2 * twos:2], lengths[2:2 + 2 * twos:2]
    margin = jnp.minimum(donor - 1, most - sink)
    moved = jax.random.randint(jax.random.fold_in(stream_key, 1), (twos,), 0, 1 << 20) % (margin + 1)
    lengths = lengths.at[1:1 + 2 * twos:2].set(donor - moved).at[2:2 + 2 * twos:2].set(sink + moved)
    return lengths[jax.random.permutation(jax.random.fold_in(stream_key, 2), number_of)]


def noise(key, shape, scale, bound, split=(), kind=jnp.bfloat16):
    loudness = steps_of(key, shape, split, -0.22, 0.18) if split else 1.0
    array = jax.random.normal(key, shape, jnp.float32) * scale * loudness
    return jnp.minimum(jnp.maximum(array, -bound), bound).astype(kind)


def bell_draw_with(stream_key, dims, deviation, limit, cuts, heavy, dtype=jnp.bfloat16):
    values = deviation * jax.random.normal(stream_key, dims, jnp.float32)
    if cuts:
        values = values * steps_of(stream_key, dims, cuts, -0.22, 0.18)
    return jnp.clip(strengthened(values, jax.random.fold_in(stream_key, 3), *heavy), -limit, limit).astype(dtype)


def setup_inputs(seed: int = 0) -> dict:
    seeds = jax.random.split(jax.random.key(seed), 18)
    return {
        "layer_input": bell_draw_with(seeds[0], (ROWS, L, D), 1.0, 6.0, ((0, 16), (1, 2)), (0, 2, 16, 2.0)),
        "segment_ids": jax.vmap(lambda own: jnp.searchsorted(jnp.cumsum(uneven_parts(own, SEGS, L, SEG_MOST, 1)), jnp.arange(L), side="right"))(jax.random.split(seeds[1], ROWS)).reshape((ROWS, L)).astype(jnp.int32),
        "key_valid": plant((jax.random.randint(seeds[2], (ROWS, L), 0, 8) < 7).astype(jnp.int32), jax.random.fold_in(seeds[2], 1), 0, 1),
        "first_gain": jnp.clip(1.0 + 0.15 * jax.random.normal(seeds[3], (LAYERS, D), jnp.float32), 0.25, 1.75).astype(jnp.bfloat16),
        "first_shift": noise(seeds[4], (LAYERS, D), 0.3, 1.75, ((1, 16),)),
        "input_weight": noise(seeds[5], (LAYERS, D, 3 * D), D ** -0.5, 0.21875, ((1, 16),)),
        "query_bias": noise(seeds[6], (LAYERS, D), 0.5, 3.0, ((1, 16),)),
        "value_bias": noise(seeds[7], (LAYERS, D), 0.5, 3.0, ((1, 16),)),
        "output_weight": noise(seeds[8], (LAYERS, D, D), (D // 32) ** -0.5, 1.25, ((1, 16),)),
        "output_bias": noise(seeds[9], (LAYERS, D), 0.3, 1.75, ((1, 16),)),
        "second_gain": jnp.clip(1.0 + 0.15 * jax.random.normal(seeds[10], (LAYERS, D), jnp.float32), 0.25, 1.75).astype(jnp.bfloat16),
        "second_shift": noise(seeds[11], (LAYERS, D), 0.3, 1.75, ((1, 16),)),
        "up_weight": noise(seeds[12], (LAYERS, D, FF), D ** -0.5, 0.21875, ((1, 16),)),
        "up_bias": noise(seeds[13], (LAYERS, FF), 0.5, 3.0, ((1, 16),)),
        "down_weight": noise(seeds[14], (LAYERS, FF, D), FF ** -0.5, 0.109375, ((1, 16),)),
        "down_bias": noise(seeds[15], (LAYERS, D), 0.3, 1.75, ((1, 16),)),
        "output_cotangent": bell_draw_with(seeds[16], (ROWS, L, D), 1.0, 6.0, ((0, 16), (1, 2)), (0, 2, 16, 2.0)),
    }


EPS = 1e-06
NEG = -1e+30

@jax.custom_vjp
def low(v):
    return lax.optimization_barrier(v.astype(jnp.bfloat16)).astype(jnp.float32)

@jax.custom_vjp
def low_back(v):
    return v

def low_keep(v):
    return (low(v), None)

def low_pass(kept, grad):
    return (grad,)

def back_keep(v):
    return (v, None)

def back_low(kept, grad):
    return (low(grad),)
low.defvjp(low_keep, low_pass)
low_back.defvjp(back_keep, back_low)

def high_dot(left_side, right_side):
    return jnp.dot(left_side, right_side, precision=lax.Precision.HIGHEST)

def layer_norm(values, norm_gain, norm_shift):
    center = values - lax.optimization_barrier(jnp.mean(values, axis=-1, keepdims=True))
    spread = lax.optimization_barrier(jnp.mean(center * center, axis=-1, keepdims=True))
    return center * lax.rsqrt(spread + EPS) * norm_gain + norm_shift

def gelu_exact(values):
    return 0.5 * values * (1.0 + lax.erf(values * 2.0 ** (-0.5)))

def attend_row(queries, keys_in, values_in, segment_row, valid_row):
    scores = jnp.einsum('qhd,khd->hqk', queries, keys_in, precision=lax.Precision.HIGHEST) * HD ** (-0.5)
    scores = low_back(scores)
    places = jnp.arange(L)
    allowed = (segment_row[:, None] == segment_row[None, :]) & ((valid_row[None, :] == 1) | (places[:, None] == places[None, :]))
    scores = jnp.where(allowed[None], scores, NEG)
    row_max = lax.optimization_barrier(jnp.max(scores, axis=-1, keepdims=True))
    expo_terms = jnp.exp(scores - row_max)
    chances = low(expo_terms / lax.optimization_barrier(jnp.sum(expo_terms, axis=-1, keepdims=True)))
    return jnp.einsum('hqk,khd->qhd', chances, values_in, precision=lax.Precision.HIGHEST)

def attend_packed(packed):
    return attend_row(packed[0], packed[1], packed[2], packed[3], packed[4])

def forward(stream, params, segment_ids, key_valid):
    first_gain, first_shift, input_weight, query_bias, value_bias, output_weight, output_bias, second_gain, second_shift, up_weight, up_bias, down_weight, down_bias = params
    row_count = stream.shape[0]
    for depth_index in range(LAYERS):
        normed = low(layer_norm(stream, first_gain[depth_index], first_shift[depth_index]))
        bias_full = jnp.concatenate([query_bias[depth_index], jnp.zeros((D,), jnp.float32), value_bias[depth_index]])
        mixed = low(low_back(high_dot(normed, input_weight[depth_index]) + bias_full))
        mixed = mixed.reshape(row_count, L, 3, H, HD)
        attended = lax.map(jax.checkpoint(attend_packed), (mixed[:, :, 0], mixed[:, :, 1], mixed[:, :, 2], segment_ids, key_valid))
        attended = low(low_back(attended.reshape(row_count, L, D)))
        stream = stream + low_back(high_dot(attended, output_weight[depth_index]) + output_bias[depth_index])
        normed_two = low(layer_norm(stream, second_gain[depth_index], second_shift[depth_index]))
        before = low_back(high_dot(normed_two, up_weight[depth_index]) + up_bias[depth_index])
        hidden = low(gelu_exact(before))
        stream = stream + low_back(high_dot(hidden, down_weight[depth_index]) + down_bias[depth_index])
    return stream

def reference(layer_input, segment_ids, key_valid, first_gain, first_shift, input_weight, query_bias, value_bias, output_weight, output_bias, second_gain, second_shift, up_weight, up_bias, down_weight, down_bias, output_cotangent):
    params = (first_gain.astype(jnp.float32), first_shift.astype(jnp.float32), input_weight.astype(jnp.float32), query_bias.astype(jnp.float32), value_bias.astype(jnp.float32), output_weight.astype(jnp.float32), output_bias.astype(jnp.float32), second_gain.astype(jnp.float32), second_shift.astype(jnp.float32), up_weight.astype(jnp.float32), up_bias.astype(jnp.float32), down_weight.astype(jnp.float32), down_bias.astype(jnp.float32))
    stream = layer_input.astype(jnp.float32)

    def apply_layers(stream_in, params_in):
        return forward(stream_in, params_in, segment_ids, key_valid)
    result, pullback = jax.vjp(apply_layers, stream, params)
    input_grad, param_grads = pullback(output_cotangent.astype(jnp.float32))
    return (result.astype(jnp.bfloat16), input_grad, param_grads[0], param_grads[1], param_grads[2], param_grads[3], param_grads[4], param_grads[5], param_grads[6], param_grads[7], param_grads[8], param_grads[9], param_grads[10], param_grads[11], param_grads[12])
```

```python
import jax
import jax.numpy as jnp
from jax import lax
from jax.experimental import pallas as pl
from jax.experimental.pallas import tpu as pltpu
from jax.sharding import PartitionSpec as P

D = 768
HD = 64
FF = 3072
LAYERS = 2
PAIR = 128
PAIRS = D // PAIR
HALF = 256

EPS = 1e-06
NEG = -1e30
F32 = jnp.float32
BF16 = jnp.bfloat16


def layer_norm(values, norm_gain, norm_shift):
    center = values - jnp.mean(values, axis=-1, keepdims=True)
    spread = jnp.mean(center * center, axis=-1, keepdims=True)
    return center * lax.rsqrt(spread + EPS) * norm_gain + norm_shift


def gelu_exact(values):
    return 0.5 * values * (1.0 + lax.erf(values * 2.0 ** (-0.5)))


def gelu_slope(values):
    return 0.5 * (1.0 + lax.erf(values * 2.0 ** (-0.5))) + values * (
        jnp.exp(-0.5 * values * values) * (2.0 * jnp.pi) ** (-0.5)
    )


def dot(left_side, right_side):
    return jnp.dot(left_side, right_side, preferred_element_type=F32)


def dot_rows(left_side, right_side):
    return lax.dot_general(left_side, right_side, (((0,), (0,)), ((), ())), preferred_element_type=F32)


def dot_back(left_side, right_side):
    return lax.dot_general(left_side, right_side, (((1,), (1,)), ((), ())), preferred_element_type=F32)


def column_sum(values):
    return dot(jnp.ones((8, values.shape[0]), BF16), values)[0]


def attend_kernel(seg_col, seg_row, valid_row, q_ref, kv_ref, halo_ref, out_ref, lse_ref, bias):
    @pl.when(pl.program_id(0) == 0)
    def _():
        rows = lax.broadcasted_iota(jnp.int32, bias.shape, 0)
        columns = lax.broadcasted_iota(jnp.int32, bias.shape, 1)
        allowed = (seg_col[...] == seg_row[...]) & ((valid_row[...] == 1) | (rows == columns))
        bias[...] = jnp.where(allowed, 0.0, NEG)

    lane = lax.broadcasted_iota(jnp.int32, (HALF, PAIR), 1)
    keys, values = kv_ref[:, :PAIR], kv_ref[:, PAIR:]
    halo_keys, halo_values = halo_ref[:, :PAIR], halo_ref[:, PAIR:]
    for block in range(2):
        rows = slice(block * HALF, (block + 1) * HALF)
        queries = q_ref[rows, :] * jnp.asarray(HD ** (-0.5), BF16)
        merged = None
        for head in range(2):
            mine = (lane // HD) == head
            query = jnp.where(mine, queries, jnp.zeros_like(queries))
            scores = dot_back(query, keys) + bias[rows, : 2 * HALF]
            top = jnp.max(scores, axis=1, keepdims=True)
            if block == 0:
                halo_scores = dot_back(query, halo_keys) + bias[rows, 2 * HALF :]
                top = jnp.maximum(top, jnp.max(halo_scores, axis=1, keepdims=True))
            terms = jnp.exp(scores - top)
            total = jnp.sum(terms, axis=1, keepdims=True)
            found = dot(terms.astype(BF16), values)
            if block == 0:
                halo_terms = jnp.exp(halo_scores - top)
                total = total + jnp.sum(halo_terms, axis=1, keepdims=True)
                found = found + dot(halo_terms.astype(BF16), halo_values)
            found = found * (1.0 / total)
            merged = found if merged is None else jnp.where(mine, found, merged)
            lse = jnp.broadcast_to(top + jnp.log(total), (HALF, PAIR))
            lse_ref[0, head : head + 1, rows] = lse.T[:1, :]
        out_ref[rows, :] = merged.astype(BF16)


def attend(segment, valid, queries, pairs, halo_pairs):
    rows, reach = queries.shape[0], segment.shape[0]
    whole = lambda shape: pl.BlockSpec(shape, lambda i: (0, 0))
    return pl.pallas_call(
        attend_kernel,
        grid=(PAIRS,),
        in_specs=[
            whole((rows, 1)),
            whole((1, reach)),
            whole((1, reach)),
            pl.BlockSpec((rows, PAIR), lambda i: (0, i)),
            pl.BlockSpec((rows, 2 * PAIR), lambda i: (0, i)),
            pl.BlockSpec((HALF, 2 * PAIR), lambda i: (0, i)),
        ],
        out_specs=[
            pl.BlockSpec((rows, PAIR), lambda i: (0, i)),
            pl.BlockSpec((1, 2, rows), lambda i: (i, 0, 0)),
        ],
        out_shape=[
            jax.ShapeDtypeStruct((rows, D), BF16),
            jax.ShapeDtypeStruct((PAIRS, 2, rows), F32),
        ],
        scratch_shapes=[pltpu.VMEM((rows, reach), F32)],
        cost_estimate=pl.CostEstimate(flops=4 * 5 * 65536 * D, bytes_accessed=6 << 20, transcendentals=5 * 65536 * 12),
        name="attend",
    )(segment[:rows, None], segment[None, :], valid[None, :], queries, pairs, halo_pairs)


def attend_back_kernel(
    seg_row, seg_col, valid_col, q_ref, kv_ref, halo_ref, grad_ref, lse_ref, dq_ref, dkv_ref, dhalo_ref, bias
):
    @pl.when(pl.program_id(0) == 0)
    def _():
        rows = lax.broadcasted_iota(jnp.int32, bias.shape, 0)
        columns = lax.broadcasted_iota(jnp.int32, bias.shape, 1)
        allowed = (seg_col[...] == seg_row[...]) & ((valid_col[...] == 1) | (rows == columns))
        bias[...] = jnp.where(allowed, 0.0, NEG)

    lane = lax.broadcasted_iota(jnp.int32, (HALF, PAIR), 1)
    keys, values = kv_ref[:, :PAIR], kv_ref[:, PAIR:]
    halo_keys, halo_values = halo_ref[:, :PAIR], halo_ref[:, PAIR:]
    keys_t, halo_keys_t = keys.T, halo_keys.T
    scale = jnp.asarray(HD ** (-0.5), BF16)
    dk = dv = dk_halo = dv_halo = None
    plus = lambda total, term: term if total is None else total + term
    for block in range(2):
        rows = slice(block * HALF, (block + 1) * HALF)
        queries = q_ref[rows, :] * scale
        grads = grad_ref[rows, :]
        dq_parts = []
        for head in range(2):
            mine = (lane // HD) == head
            query = jnp.where(mine, queries, jnp.zeros_like(queries))
            grad = jnp.where(mine, grads, jnp.zeros_like(grads))
            lse = lse_ref[0, head : head + 1, rows]
            dims = slice(head * HD, (head + 1) * HD)
            chances = jnp.exp(dot_back(keys, query) + bias[: 2 * HALF, rows] - lse)
            back = dot_back(values, grad)
            inner = jnp.sum(chances * back, axis=0, keepdims=True)
            if block == 0:
                halo_chances = jnp.exp(dot_back(halo_keys, query) + bias[2 * HALF :, rows] - lse)
                halo_back = dot_back(halo_values, grad)
                inner = inner + jnp.sum(halo_chances * halo_back, axis=0, keepdims=True)
            slopes = (chances * (back - inner)).astype(BF16)
            dq = dot(keys_t[dims, :], slopes)
            dk = plus(dk, dot(slopes, query))
            dv = plus(dv, dot(chances.astype(BF16), grad))
            if block == 0:
                halo_slopes = (halo_chances * (halo_back - inner)).astype(BF16)
                dq = dq + dot(halo_keys_t[dims, :], halo_slopes)
                dk_halo = plus(dk_halo, dot(halo_slopes, query))
                dv_halo = plus(dv_halo, dot(halo_chances.astype(BF16), grad))
            dq_parts.append(dq)
        dq = jnp.concatenate(dq_parts, axis=0).T * HD ** (-0.5)
        dq_ref[rows, :] = dq.astype(BF16)
    dkv_ref[:, :PAIR] = dk.astype(BF16)
    dkv_ref[:, PAIR:] = dv.astype(BF16)
    dhalo_ref[:, :PAIR] = dk_halo.astype(BF16)
    dhalo_ref[:, PAIR:] = dv_halo.astype(BF16)


def attend_back(segment, valid, queries, pairs, halo_pairs, grads, lse):
    rows, reach = queries.shape[0], segment.shape[0]
    whole = lambda shape: pl.BlockSpec(shape, lambda i: (0, 0))
    tokens = pl.BlockSpec((rows, PAIR), lambda i: (0, i))
    both = pl.BlockSpec((rows, 2 * PAIR), lambda i: (0, i))
    halo = pl.BlockSpec((HALF, 2 * PAIR), lambda i: (0, i))
    return pl.pallas_call(
        attend_back_kernel,
        grid=(PAIRS,),
        in_specs=[
            whole((1, rows)),
            whole((reach, 1)),
            whole((reach, 1)),
            tokens,
            both,
            halo,
            tokens,
            pl.BlockSpec((1, 2, rows), lambda i: (i, 0, 0)),
        ],
        out_specs=[tokens, both, halo],
        out_shape=[
            jax.ShapeDtypeStruct((rows, D), BF16),
            jax.ShapeDtypeStruct((rows, 2 * D), BF16),
            jax.ShapeDtypeStruct((HALF, 2 * D), BF16),
        ],
        scratch_shapes=[pltpu.VMEM((reach, rows), F32)],
        cost_estimate=pl.CostEstimate(flops=10 * 5 * 65536 * D, bytes_accessed=10 << 20, transcendentals=5 * 65536 * 12),
        name="attend_back",
    )(segment[None, :rows], segment[:, None], valid[:, None], queries, pairs, halo_pairs, grads, lse)


def swap_seq(values):
    return lax.ppermute(values, "seq", [(0, 1), (1, 0)])


def pair_columns(matrix):
    return matrix.reshape(-1, 2, PAIRS, PAIR).swapaxes(1, 2).reshape(-1, 2 * D)


def unpair_columns(matrix):
    return matrix.reshape(-1, PAIRS, 2, PAIR).swapaxes(1, 2).reshape(-1, 2 * D)


def column_blocks(matrix):
    rows = matrix.shape[0]
    return matrix.reshape(rows, -1, D).swapaxes(0, 1).reshape(-1, D)


def local(
    layer_input,
    segment_ids,
    key_valid,
    first_gain,
    first_shift,
    input_weight,
    query_bias,
    value_bias,
    output_weight,
    output_bias,
    second_gain,
    second_shift,
    up_weight,
    up_bias,
    down_weight,
    down_bias,
    output_cotangent,
):
    right = lax.axis_index("seq") == 1
    rows_of = input_weight.shape[1]
    owners = D // rows_of

    def near_first(values):
        turned = jnp.concatenate([values[HALF:], values[:HALF]], axis=0)
        return jnp.where(right, values, turned)

    def by_block(values):
        blocks = values.reshape(4, HALF)
        return jnp.where(
            right,
            jnp.concatenate([blocks[2], blocks[3], blocks[1]]),
            jnp.concatenate([blocks[1], blocks[0], blocks[2]]),
        )

    def gather(shard):
        return lax.all_gather(shard, "fsdp", axis=0, tiled=False)

    segment, valid = by_block(segment_ids[0]), by_block(key_valid[0])

    ordered = [
        jnp.concatenate([input_weight[depth][:, :D], pair_columns(input_weight[depth][:, D:])], axis=1)
        for depth in range(LAYERS)
    ]
    smalls = [first_gain, first_shift, query_bias, value_bias, output_bias, second_gain, second_shift, down_bias]
    small = jnp.concatenate(
        [member.reshape(LAYERS, 1, rows_of) for member in smalls] + [up_bias.reshape(LAYERS, 4, rows_of)], axis=1
    ).reshape(-1)
    side = rows_of * 128
    small_block = jnp.pad(small, (0, side - small.shape[0])).reshape(rows_of, 128)
    first = gather(jnp.concatenate([ordered[0], small_block], axis=1))

    def rest(depth):
        return [output_weight[depth], column_blocks(up_weight[depth]), down_weight[depth]]

    second = gather(jnp.concatenate(rest(0) + [column_blocks(ordered[1])], axis=0))
    third = gather(jnp.concatenate(rest(1), axis=0))

    def take(packed, start, count):
        part = packed[:, start * rows_of : (start + count) * rows_of]
        return part

    def joined(packed, start, count):
        return jnp.concatenate(
            [take(packed, start + j, 1).reshape(D, D) for j in range(count)], axis=1
        )

    def unpacked(packed):
        return take(packed, 0, 1).reshape(D, D), joined(packed, 1, 4), take(packed, 5, 4).reshape(FF, D)

    first = first.reshape(D, -1)
    mix_weights = [first[:, : 3 * D], joined(second, 9, 3)]
    mlp_weights = [unpacked(second), unpacked(third)]
    smalls_full = (
        first[:, 3 * D :].reshape(owners, side)[:, : small.shape[0]].reshape(owners, LAYERS, 12, rows_of).astype(F32)
    )
    vectors = smalls_full[:, :, :8].transpose(1, 2, 0, 3).reshape(LAYERS, 8, D)
    up_biases = smalls_full[:, :, 8:].transpose(1, 0, 2, 3).reshape(LAYERS, FF)

    stream = near_first(layer_input[0]).astype(F32)
    kept = []
    for depth in range(LAYERS):
        gain_one, shift_one, query_shift, value_shift, out_shift, gain_two, shift_two, fall_shift = [
            vectors[depth, j] for j in range(8)
        ]
        mix_weight = mix_weights[depth]
        out_weight, rise_weight, fall_weight = mlp_weights[depth]
        normed = layer_norm(stream, gain_one, shift_one).astype(BF16)
        halo_normed = swap_seq(normed[:HALF])
        pair_shift = jnp.stack([jnp.zeros((PAIRS, PAIR), F32), value_shift.reshape(PAIRS, PAIR)], axis=1).reshape(-1)
        queries = (dot(normed, mix_weight[:, :D]) + query_shift).astype(BF16)
        pairs = (dot(normed, mix_weight[:, D:]) + pair_shift).astype(BF16)
        halo_pairs = (dot(halo_normed, mix_weight[:, D:]) + pair_shift).astype(BF16)
        attended, lse = attend(segment, valid, queries, pairs, halo_pairs)
        stream_mid = stream + (dot(attended, out_weight) + out_shift)
        normed_two = layer_norm(stream_mid, gain_two, shift_two).astype(BF16)
        before = dot(normed_two, rise_weight) + up_biases[depth]
        hidden = gelu_exact(before).astype(BF16)
        stream_next = stream_mid + (dot(hidden, fall_weight) + fall_shift)
        kept.append((stream, normed, halo_normed, queries, pairs, halo_pairs, lse, attended, stream_mid, normed_two, before, hidden))
        stream = stream_next

    grad_stream = near_first(output_cotangent[0]).astype(F32)
    packs = {}
    small_grads = [None] * LAYERS

    def owned_rows(matrix):
        return matrix.astype(BF16).reshape(owners, -1, D)

    def owned_blocks(matrix):
        blocks = matrix.astype(BF16).reshape(owners, rows_of, -1, D)
        return blocks.swapaxes(1, 2).reshape(owners, -1, D)

    for depth in reversed(range(LAYERS)):
        gain_one, shift_one, query_shift, value_shift, out_shift, gain_two, shift_two, fall_shift = [
            vectors[depth, j] for j in range(8)
        ]
        mix_weight = mix_weights[depth]
        out_weight, rise_weight, fall_weight = mlp_weights[depth]
        (stream_in, normed, halo_normed, queries, pairs, halo_pairs, lse, attended, stream_mid, normed_two, before, hidden) = kept[depth]
        grad_fall = grad_stream.astype(BF16)
        fall_weight_grad = dot_rows(hidden, grad_fall)
        fall_shift_grad = column_sum(grad_fall)
        grad_before = (dot_back(grad_fall, fall_weight) * gelu_slope(before)).astype(BF16)
        rise_weight_grad = dot_rows(normed_two, grad_before)
        rise_shift_grad = column_sum(grad_before)
        grad_normed_two = dot_back(grad_before, rise_weight)
        norm_pair_two = jax.vjp(layer_norm, stream_mid, gain_two, shift_two)
        grad_mid_norm, gain_two_grad, shift_two_grad = norm_pair_two[1](grad_normed_two)
        grad_mid = grad_stream + grad_mid_norm
        grad_branch = grad_mid.astype(BF16)
        out_weight_grad = dot_rows(attended, grad_branch)
        out_shift_grad = column_sum(grad_branch)
        grad_attended = dot_back(grad_branch, out_weight).astype(BF16)
        dq, dpairs, dhalo = attend_back(segment, valid, queries, pairs, halo_pairs, grad_attended, lse)
        halo_back = swap_seq(dot_back(dhalo, mix_weight[:, D:]).astype(BF16)).astype(F32)
        normed_all = jnp.concatenate([normed, halo_normed], axis=0)
        dpairs_all = jnp.concatenate([dpairs, dhalo], axis=0)
        query_weight_grad = dot_rows(normed, dq)
        pair_weight_grad = dot_rows(normed_all, dpairs_all)
        query_shift_grad = column_sum(dq)
        value_shift_grad = column_sum(dpairs_all).reshape(PAIRS, 2, PAIR)[:, 1].reshape(D)
        grad_normed = dot_back(dq, mix_weight[:, :D]) + dot_back(dpairs, mix_weight[:, D:])
        grad_normed = jnp.concatenate([grad_normed[:HALF] + halo_back, grad_normed[HALF:]], axis=0)
        norm_pair_one = jax.vjp(layer_norm, stream_in, gain_one, shift_one)
        grad_in_norm, gain_one_grad, shift_one_grad = norm_pair_one[1](grad_normed)
        grad_stream = grad_mid + grad_in_norm
        packs["fall", depth] = owned_rows(fall_weight_grad)
        packs["rise", depth] = owned_blocks(rise_weight_grad)
        packs["out", depth] = owned_rows(out_weight_grad)
        packs["query", depth] = owned_rows(query_weight_grad)
        packs["pair", depth] = owned_blocks(pair_weight_grad)
        small_grads[depth] = jnp.concatenate(
            [
                member.reshape(owners, 1, rows_of)
                for member in (
                    gain_one_grad,
                    shift_one_grad,
                    query_shift_grad,
                    value_shift_grad,
                    out_shift_grad,
                    gain_two_grad,
                    shift_two_grad,
                    fall_shift_grad,
                )
            ]
            + [rise_shift_grad.reshape(owners, 4, rows_of)],
            axis=1,
        )

    small_all = jnp.concatenate(small_grads, axis=1).astype(BF16).reshape(owners, -1)
    small_all = jnp.pad(small_all, ((0, 0), (0, 16 * D - small_all.shape[1]))).reshape(owners, 16, D)

    def reduced(names):
        parts = [packs[name] for name in names]
        mine = lax.psum_scatter(jnp.concatenate(parts, axis=1), "fsdp", scatter_dimension=0, tiled=False)
        total = mine.astype(F32) + swap_seq(mine).astype(F32)
        found, at = {}, 0
        for name, part in zip(names, parts):
            found[name] = total[at : at + part.shape[1]]
            at += part.shape[1]
        return found

    packs["small", 0] = small_all
    sums = reduced([("fall", 1), ("rise", 1)])
    sums.update(reduced([("out", 1), ("query", 1), ("pair", 1), ("fall", 0), ("rise", 0)]))
    sums.update(reduced([("out", 0), ("query", 0), ("pair", 0), ("small", 0)]))

    def columns(block_rows, count):
        return block_rows.reshape(count, rows_of, D).swapaxes(0, 1).reshape(rows_of, count * D)

    def both(fn):
        return jnp.stack([fn(depth) for depth in range(LAYERS)])

    small_sum = sums["small", 0].reshape(-1)[: small.shape[0]].reshape(LAYERS, 12, rows_of)
    mix_out = both(
        lambda depth: jnp.concatenate(
            [sums["query", depth], unpair_columns(columns(sums["pair", depth], 2))], axis=1
        )
    )
    layer_output = near_first(stream.astype(BF16))[None]
    input_grad = near_first(grad_stream)[None]
    return (
        layer_output,
        input_grad,
        small_sum[:, 0],
        small_sum[:, 1],
        mix_out,
        small_sum[:, 2],
        small_sum[:, 3],
        both(lambda depth: sums["out", depth]),
        small_sum[:, 4],
        small_sum[:, 5],
        small_sum[:, 6],
        both(lambda depth: columns(sums["rise", depth], 4)),
        small_sum[:, 8:].reshape(LAYERS, 4 * rows_of),
        both(lambda depth: sums["fall", depth]),
        small_sum[:, 7],
    )


def solution(mesh):
    vector, matrix = P(None, "fsdp"), P(None, "fsdp", None)
    tokens, places = P("fsdp", "seq", None), P("fsdp", None)
    return jax.shard_map(
        local,
        mesh=mesh,
        in_specs=(
            tokens,
            places,
            places,
            vector,
            vector,
            matrix,
            vector,
            vector,
            matrix,
            vector,
            vector,
            vector,
            matrix,
            vector,
            matrix,
            vector,
            tokens,
        ),
        out_specs=(
            tokens,
            tokens,
            vector,
            vector,
            matrix,
            vector,
            vector,
            matrix,
            vector,
            vector,
            vector,
            matrix,
            vector,
            matrix,
            vector,
        ),
        check_vma=False,
    )
```

```python
import jax
import jax.numpy as jnp
from jax import lax
from jax.experimental import pallas as pl
from jax.experimental.pallas import tpu as pltpu
from jax.sharding import PartitionSpec as P

D = 768
HD = 64
FF = 3072
LAYERS = 2
PAIR = 128
PAIRS = D // PAIR
HALF = 256

EPS = 1e-06
NEG = -1e30
F32 = jnp.float32
BF16 = jnp.bfloat16


def layer_norm(values, norm_gain, norm_shift):
    center = values - jnp.mean(values, axis=-1, keepdims=True)
    spread = jnp.mean(center * center, axis=-1, keepdims=True)
    return center * lax.rsqrt(spread + EPS) * norm_gain + norm_shift


def gelu_exact(values):
    return 0.5 * values * (1.0 + lax.erf(values * 2.0 ** (-0.5)))


def gelu_slope(values):
    return 0.5 * (1.0 + lax.erf(values * 2.0 ** (-0.5))) + values * (
        jnp.exp(-0.5 * values * values) * (2.0 * jnp.pi) ** (-0.5)
    )


def dot(left_side, right_side):
    return jnp.dot(left_side, right_side, preferred_element_type=F32)


def dot_rows(left_side, right_side):
    return lax.dot_general(left_side, right_side, (((0,), (0,)), ((), ())), preferred_element_type=F32)


def dot_back(left_side, right_side):
    return lax.dot_general(left_side, right_side, (((1,), (1,)), ((), ())), preferred_element_type=F32)


def column_sum(values):
    return dot(jnp.ones((8, values.shape[0]), BF16), values)[0]


def attend_kernel(seg_col, seg_row, valid_row, q_ref, kv_ref, halo_ref, out_ref, lse_ref, bias):
    @pl.when(pl.program_id(0) == 0)
    def _():
        rows = lax.broadcasted_iota(jnp.int32, bias.shape, 0)
        columns = lax.broadcasted_iota(jnp.int32, bias.shape, 1)
        allowed = (seg_col[...] == seg_row[...]) & ((valid_row[...] == 1) | (rows == columns))
        bias[...] = jnp.where(allowed, 0.0, NEG)

    lane = lax.broadcasted_iota(jnp.int32, (HALF, PAIR), 1)
    keys, values = kv_ref[:, :PAIR], kv_ref[:, PAIR:]
    halo_keys, halo_values = halo_ref[:, :PAIR], halo_ref[:, PAIR:]
    for block in range(2):
        rows = slice(block * HALF, (block + 1) * HALF)
        queries = q_ref[rows, :] * jnp.asarray(HD ** (-0.5), BF16)
        merged = None
        for head in range(2):
            mine = (lane // HD) == head
            query = jnp.where(mine, queries, jnp.zeros_like(queries))
            scores = dot_back(query, keys) + bias[rows, : 2 * HALF]
            top = jnp.max(scores, axis=1, keepdims=True)
            if block == 0:
                halo_scores = dot_back(query, halo_keys) + bias[rows, 2 * HALF :]
                top = jnp.maximum(top, jnp.max(halo_scores, axis=1, keepdims=True))
            terms = jnp.exp(scores - top)
            total = jnp.sum(terms, axis=1, keepdims=True)
            found = dot(terms.astype(BF16), values)
            if block == 0:
                halo_terms = jnp.exp(halo_scores - top)
                total = total + jnp.sum(halo_terms, axis=1, keepdims=True)
                found = found + dot(halo_terms.astype(BF16), halo_values)
            found = found * (1.0 / total)
            merged = found if merged is None else jnp.where(mine, found, merged)
            lse = jnp.broadcast_to(top + jnp.log(total), (HALF, PAIR))
            lse_ref[0, head : head + 1, rows] = lse.T[:1, :]
        out_ref[rows, :] = merged.astype(BF16)


def attend(segment, valid, queries, pairs, halo_pairs):
    rows, reach = queries.shape[0], segment.shape[0]
    whole = lambda shape: pl.BlockSpec(shape, lambda i: (0, 0))
    return pl.pallas_call(
        attend_kernel,
        grid=(PAIRS,),
        in_specs=[
            whole((rows, 1)),
            whole((1, reach)),
            whole((1, reach)),
            pl.BlockSpec((rows, PAIR), lambda i: (0, i)),
            pl.BlockSpec((rows, 2 * PAIR), lambda i: (0, i)),
            pl.BlockSpec((HALF, 2 * PAIR), lambda i: (0, i)),
        ],
        out_specs=[
            pl.BlockSpec((rows, PAIR), lambda i: (0, i)),
            pl.BlockSpec((1, 2, rows), lambda i: (i, 0, 0)),
        ],
        out_shape=[
            jax.ShapeDtypeStruct((rows, D), BF16),
            jax.ShapeDtypeStruct((PAIRS, 2, rows), F32),
        ],
        scratch_shapes=[pltpu.VMEM((rows, reach), F32)],
        cost_estimate=pl.CostEstimate(flops=4 * 5 * 65536 * D, bytes_accessed=6 << 20, transcendentals=5 * 65536 * 12),
        name="attend",
    )(segment[:rows, None], segment[None, :], valid[None, :], queries, pairs, halo_pairs)


def attend_back_kernel(
    seg_row, seg_col, valid_col, q_ref, kv_ref, halo_ref, grad_ref, lse_ref, _, dq_ref, dkv_ref, dhalo_ref, bias
):
    @pl.when(pl.program_id(0) == 0)
    def _():
        rows = lax.broadcasted_iota(jnp.int32, bias.shape, 0)
        columns = lax.broadcasted_iota(jnp.int32, bias.shape, 1)
        allowed = (seg_col[...] == seg_row[...]) & ((valid_col[...] == 1) | (rows == columns))
        bias[...] = jnp.where(allowed, 0.0, NEG)

    lane = lax.broadcasted_iota(jnp.int32, (HALF, PAIR), 1)
    keys, values = kv_ref[:, :PAIR], kv_ref[:, PAIR:]
    halo_keys, halo_values = halo_ref[:, :PAIR], halo_ref[:, PAIR:]
    keys_t, halo_keys_t = keys.T, halo_keys.T
    scale = jnp.asarray(HD ** (-0.5), BF16)
    dk = dv = dk_halo = dv_halo = None
    plus = lambda total, term: term if total is None else total + term
    for block in range(2):
        rows = slice(block * HALF, (block + 1) * HALF)
        queries = q_ref[rows, :] * scale
        grads = grad_ref[rows, :]
        dq_parts = []
        for head in range(2):
            mine = (lane // HD) == head
            query = jnp.where(mine, queries, jnp.zeros_like(queries))
            grad = jnp.where(mine, grads, jnp.zeros_like(grads))
            lse = lse_ref[0, head : head + 1, rows]
            dims = slice(head * HD, (head + 1) * HD)
            chances = jnp.exp(dot_back(keys, query) + bias[: 2 * HALF, rows] - lse)
            back = dot_back(values, grad)
            inner = jnp.sum(chances * back, axis=0, keepdims=True)
            if block == 0:
                halo_chances = jnp.exp(dot_back(halo_keys, query) + bias[2 * HALF :, rows] - lse)
                halo_back = dot_back(halo_values, grad)
                inner = inner + jnp.sum(halo_chances * halo_back, axis=0, keepdims=True)
            slopes = (chances * (back - inner)).astype(BF16)
            dq = dot(keys_t[dims, :], slopes)
            dk = plus(dk, dot(slopes, query))
            dv = plus(dv, dot(chances.astype(BF16), grad))
            if block == 0:
                halo_slopes = (halo_chances * (halo_back - inner)).astype(BF16)
                dq = dq + dot(halo_keys_t[dims, :], halo_slopes)
                dk_halo = plus(dk_halo, dot(halo_slopes, query))
                dv_halo = plus(dv_halo, dot(halo_chances.astype(BF16), grad))
            dq_parts.append(dq)
        dq = jnp.concatenate(dq_parts, axis=0).T * HD ** (-0.5)
        dq_ref[rows, :] = dq.astype(BF16)
    dkv_ref[:, :PAIR] = dk.astype(BF16)
    dkv_ref[:, PAIR:] = dv.astype(BF16)
    dhalo_ref[:, :PAIR] = dk_halo.astype(BF16)
    dhalo_ref[:, PAIR:] = dv_halo.astype(BF16)


def attend_back(segment, valid, queries, pairs, halo_pairs, grads, lse, earlier):
    rows, reach = queries.shape[0], segment.shape[0]
    whole = lambda shape: pl.BlockSpec(shape, lambda i: (0, 0))
    tokens = pl.BlockSpec((rows, PAIR), lambda i: (0, i))
    both = pl.BlockSpec((rows, 2 * PAIR), lambda i: (0, i))
    halo = pl.BlockSpec((HALF, 2 * PAIR), lambda i: (0, i))
    return pl.pallas_call(
        attend_back_kernel,
        grid=(PAIRS,),
        in_specs=[
            whole((1, rows)),
            whole((reach, 1)),
            whole((reach, 1)),
            tokens,
            both,
            halo,
            tokens,
            pl.BlockSpec((1, 2, rows), lambda i: (i, 0, 0)),
            pl.BlockSpec(memory_space=pl.ANY),
        ],
        out_specs=[tokens, both, halo],
        out_shape=[
            jax.ShapeDtypeStruct((rows, D), BF16),
            jax.ShapeDtypeStruct((rows, 2 * D), BF16),
            jax.ShapeDtypeStruct((HALF, 2 * D), BF16),
        ],
        scratch_shapes=[pltpu.VMEM((reach, rows), F32)],
        cost_estimate=pl.CostEstimate(flops=10 * 5 * 65536 * D, bytes_accessed=10 << 20, transcendentals=5 * 65536 * 12),
        name="attend_back",
    )(segment[None, :rows], segment[:, None], valid[:, None], queries, pairs, halo_pairs, grads, lse, earlier)


def swap_seq(values):
    return lax.ppermute(values, "seq", [(0, 1), (1, 0)])


def pair_columns(matrix):
    return matrix.reshape(-1, 2, PAIRS, PAIR).swapaxes(1, 2).reshape(-1, 2 * D)


def unpair_columns(matrix):
    return matrix.reshape(-1, PAIRS, 2, PAIR).swapaxes(1, 2).reshape(-1, 2 * D)


HOPS = 16


def place(z, y, core):
    return (z * 2 + y) * 2 + core


def hop(values, target):
    pairs = []
    for z in range(4):
        for y in range(2):
            for core in range(2):
                goal = target(z, y, core)
                if goal is not None:
                    pairs.append((place(z, y, core), place(*goal)))
    return lax.ppermute(values, "fsdp", pairs)


def hop_core(values):
    return hop(values, lambda z, y, core: (z, y, 1 - core))


def hop_y(values):
    return hop(values, lambda z, y, core: (z, 1 - y, core))


def hop_z(values, table):
    return hop(values, lambda z, y, core: None if z not in table else (table[z], y, core))


def up(values, sources=(0, 1, 2)):
    return hop(values, lambda z, y, core: (z + 1, y, core) if z in sources else None)


def down(values, sources=(1, 2, 3)):
    return hop(values, lambda z, y, core: (z - 1, y, core) if z in sources else None)


def pick(values, index, axis):
    return lax.dynamic_index_in_dim(values, index, axis, keepdims=False)


def half_of(values, x):
    half = values.shape[-1] // 2
    return lax.dynamic_slice_in_dim(values, x * half, half, axis=values.ndim - 1)


def side_by_side(blocks):
    rows = D // HOPS
    count = blocks.shape[-2] // rows
    return jnp.concatenate([blocks[..., j * rows : (j + 1) * rows, :] for j in range(count)], axis=-1)


def gather_hops(rise_shard, fall_shard, name):
    x = lax.axis_index("seq")
    with jax.named_scope(name):
        mine = jnp.concatenate([half_of(rise_shard, x), side_by_side(half_of(fall_shard, x))], axis=1)
        with jax.named_scope("up1"):
            up_one = up(mine)
        with jax.named_scope("down1"):
            down_one = down(mine)
        with jax.named_scope("up2"):
            up_two = up(up_one, (1, 2))
        with jax.named_scope("down2"):
            down_two = down(down_one, (1, 2))
        with jax.named_scope("up3"):
            up_three = up(up_two, (2,))
        with jax.named_scope("down3"):
            down_three = down(down_two, (1,))
        line = jnp.stack([mine, down_one + up_three, down_two + up_two, down_three + up_one])
        split = mine.shape[1] // 2
        line_a, line_b = line[:, :, :split], line[:, :, split:]
        with jax.named_scope("y1"):
            first_a = jnp.concatenate([line_a, hop_y(line_a)], axis=0)
        with jax.named_scope("x1"):
            first_b = jnp.concatenate([line_b, swap_seq(line_b)], axis=0)
        with jax.named_scope("x2"):
            second_a = swap_seq(first_a)
        with jax.named_scope("y2"):
            second_b = hop_y(first_b)
        with jax.named_scope("c1"):
            third_a = hop_core(first_a)
        with jax.named_scope("c2"):
            third_b = hop_core(first_b)
        with jax.named_scope("c3"):
            fourth_a = hop_core(second_a)
        with jax.named_scope("c4"):
            fourth_b = hop_core(second_b)
    return [first_a, second_a, third_a, fourth_a, first_b, second_b, third_b, fourth_b]


def along_z(line, name):
    z = lax.axis_index("fsdp") // 4
    rising = falling = None
    with jax.named_scope(name):
        for step in (3, 2, 1):
            low, high = pick(line, jnp.minimum(z + step, 3), 0), pick(line, jnp.maximum(z - step, 0), 0)
            with jax.named_scope(f"up{step}"):
                rising = up(low if rising is None else low + rising, tuple(range(4 - step)))
            with jax.named_scope(f"down{step}"):
                falling = down(high if falling is None else high + falling, tuple(range(step, 4)))
        return (pick(line, z, 0).astype(F32) + rising.astype(F32) + falling.astype(F32)).astype(BF16)


def reduce_core(matrix):
    core = lax.axis_index("fsdp") % 2
    both = matrix.reshape(8, 2, -1, matrix.shape[-1])
    return [pick(both, core, 1), hop_core(pick(both, 1 - core, 1))]


def total(terms):
    result = terms[0].astype(F32)
    for term in terms[1:]:
        result = result + term.astype(F32)
    return result.astype(BF16)


def sent_x(terms):
    x = lax.axis_index("seq")
    return [half_of(term, x) for term in terms] + [swap_seq(total([half_of(term, 1 - x) for term in terms]))]


def sent_y(terms):
    y = (lax.axis_index("fsdp") // 2) % 2
    terms = [term.reshape((4, 2) + term.shape[1:]) for term in terms]
    return [pick(term, y, 1) for term in terms] + [hop_y(total([pick(term, 1 - y, 1) for term in terms]))]


def reduce_line(first_x, first_y, name):
    with jax.named_scope(name):
        with jax.named_scope("x1"):
            first_x = sent_x(first_x)
        with jax.named_scope("y1"):
            first_y = sent_y(first_y)
        with jax.named_scope("y2"):
            first_x = total(sent_y(first_x))
        with jax.named_scope("x2"):
            first_y = total(sent_x(first_y))
    return first_x, first_y


def both_halves(mine, other, start, size):
    here, there = mine[:, start : start + size], other[:, start : start + size]
    left = lax.axis_index("seq") == 0
    return jnp.concatenate([jnp.where(left, here, there), jnp.where(left, there, here)], axis=1).astype(F32)


def assemble_kernel(*refs):
    sources, (rise, fall, held_rise, held_fall, in_sems, out_sems) = refs[:8], refs[-6:]
    my_x, me = lax.axis_index("seq"), lax.axis_index("fsdp")
    my_core, my_y, my_z = me % 2, (me // 2) % 2, me // 4
    z_of = [(my_z + slot) % 4 for slot in range(4)]
    rows = D // HOPS
    for index, source in enumerate(sources):
        is_rise, other_core, second = index < 4, (index % 4) // 2, index % 2
        core = (my_core + other_core) % 2
        for slot in range(8):
            turn, z = slot // 4, z_of[slot % 4]
            x = (my_x + (second if is_rise else turn)) % 2
            y = (my_y + (turn if is_rise else second)) % 2
            owner = (z * 2 + y) * 2 + core
            if is_rise:
                pltpu.make_async_copy(
                    source.at[slot],
                    held_rise.at[
                        pl.ds(pl.multiple_of(owner * rows, 16), rows),
                        pl.ds(pl.multiple_of(x * (FF // 2), 128), FF // 2),
                    ],
                    in_sems.at[0],
                ).start()
                continue
            for block in range(4):
                pltpu.make_async_copy(
                    source.at[slot, :, pl.ds(block * (D // 2), D // 2)],
                    held_fall.at[
                        pl.ds(pl.multiple_of((owner * 4 + block) * rows, 16), rows),
                        pl.ds(pl.multiple_of(x * (D // 2), 128), D // 2),
                    ],
                    in_sems.at[1],
                ).start()
    for which, (held, out) in enumerate(((held_rise, rise), (held_fall, fall))):
        pltpu.make_async_copy(held, held, in_sems.at[which]).wait()
        pltpu.make_async_copy(held, out, out_sems.at[which]).start()
    for which, (held, out) in enumerate(((held_rise, rise), (held_fall, fall))):
        pltpu.make_async_copy(held, out, out_sems.at[which]).wait()


def assemble(buffers, earlier):
    shapes = [(D, FF), (FF, D)]
    return pl.pallas_call(
        assemble_kernel,
        in_specs=[pl.BlockSpec(memory_space=pl.ANY)] * 9,
        out_specs=[pl.BlockSpec(memory_space=pl.ANY)] * 2,
        out_shape=[jax.ShapeDtypeStruct(shape, BF16) for shape in shapes],
        scratch_shapes=[pltpu.VMEM(shape, BF16) for shape in shapes]
        + [pltpu.SemaphoreType.DMA((2,)), pltpu.SemaphoreType.DMA((2,))],
        compiler_params=pltpu.CompilerParams(vmem_limit_bytes=24 << 20),
        cost_estimate=pl.CostEstimate(flops=0, bytes_accessed=4 * 2 * D * FF, transcendentals=0),
        name="assemble",
    )(*buffers, earlier)


def local(
    layer_input,
    segment_ids,
    key_valid,
    first_gain,
    first_shift,
    input_weight,
    query_bias,
    value_bias,
    output_weight,
    output_bias,
    second_gain,
    second_shift,
    up_weight,
    up_bias,
    down_weight,
    down_bias,
    output_cotangent,
):
    right = lax.axis_index("seq") == 1
    rows_of = input_weight.shape[1]
    owners = D // rows_of

    def near_first(values):
        turned = jnp.concatenate([values[HALF:], values[:HALF]], axis=0)
        return jnp.where(right, values, turned)

    def by_block(values):
        blocks = values.reshape(4, HALF)
        return jnp.where(
            right,
            jnp.concatenate([blocks[2], blocks[3], blocks[1]]),
            jnp.concatenate([blocks[1], blocks[0], blocks[2]]),
        )

    def gather(shard):
        return lax.all_gather(shard, "fsdp", axis=0, tiled=False)

    segment, valid = by_block(segment_ids[0]), by_block(key_valid[0])

    smalls = [first_gain, first_shift, query_bias, value_bias, output_bias, second_gain, second_shift, down_bias]
    small = jnp.concatenate(
        [member.reshape(LAYERS, 1, rows_of) for member in smalls] + [up_bias.reshape(LAYERS, 4, rows_of)], axis=1
    ).reshape(-1)
    side = rows_of * 128
    small_block = jnp.pad(small, (0, side - small.shape[0])).reshape(rows_of, 128)

    def mixing(depth):
        return [input_weight[depth][:, :D], pair_columns(input_weight[depth][:, D:]), output_weight[depth]]

    with jax.named_scope("mixing0"):
        low = gather(jnp.concatenate(mixing(0) + [small_block], axis=1)).reshape(D, -1)
    with jax.named_scope("mixing1"):
        high = gather(jnp.concatenate(mixing(1), axis=1)).reshape(D, -1)
    mix_weights = [low[:, : 3 * D], high[:, : 3 * D]]
    out_weights = [low[:, 3 * D : 4 * D], high[:, 3 * D : 4 * D]]
    smalls_full = (
        low[:, 4 * D :].reshape(owners, side)[:, : small.shape[0]].reshape(owners, LAYERS, 12, rows_of).astype(F32)
    )
    vectors = smalls_full[:, :, :8].transpose(1, 2, 0, 3).reshape(LAYERS, 8, D)
    up_biases = smalls_full[:, :, 8:].transpose(1, 0, 2, 3).reshape(LAYERS, FF)
    by_hops = owners == HOPS
    if by_hops:
        pieces = [gather_hops(up_weight[depth], down_weight[depth], f"gather{depth}") for depth in range(LAYERS)]

    def feed_weights(depth, earlier):
        if by_hops:
            return assemble(pieces[depth], earlier)
        return gather(up_weight[depth]).reshape(D, FF), gather(down_weight[depth]).reshape(FF, D)

    stream = near_first(layer_input[0]).astype(F32)
    kept, feed = [], []
    for depth in range(LAYERS):
        gain_one, shift_one, query_shift, value_shift, out_shift, gain_two, shift_two, fall_shift = [
            vectors[depth, j] for j in range(8)
        ]
        mix_weight, out_weight = mix_weights[depth], out_weights[depth]
        normed = layer_norm(stream, gain_one, shift_one).astype(BF16)
        halo_normed = swap_seq(normed[:HALF])
        pair_shift = jnp.stack([jnp.zeros((PAIRS, PAIR), F32), value_shift.reshape(PAIRS, PAIR)], axis=1).reshape(-1)
        queries = (dot(normed, mix_weight[:, :D]) + query_shift).astype(BF16)
        pairs = (dot(normed, mix_weight[:, D:]) + pair_shift).astype(BF16)
        halo_pairs = (dot(halo_normed, mix_weight[:, D:]) + pair_shift).astype(BF16)
        attended, lse = attend(segment, valid, queries, pairs, halo_pairs)
        stream_mid = stream + (dot(attended, out_weight) + out_shift)
        normed_two = layer_norm(stream_mid, gain_two, shift_two).astype(BF16)
        rise_weight, fall_weight = feed_weights(depth, attended)
        feed.append((rise_weight, fall_weight))
        before = dot(normed_two, rise_weight) + up_biases[depth]
        hidden = gelu_exact(before).astype(BF16)
        stream_next = stream_mid + (dot(hidden, fall_weight) + fall_shift)
        kept.append((stream, normed, halo_normed, queries, pairs, halo_pairs, lse, attended, stream_mid, normed_two, before, hidden))
        stream = stream_next

    grad_stream = near_first(output_cotangent[0]).astype(F32)
    small_grads = [None] * LAYERS

    def scattered(matrix):
        return lax.psum_scatter(matrix, "fsdp", scatter_dimension=0, tiled=True)

    def over_seq(mine):
        return mine.astype(F32) + swap_seq(mine).astype(F32)

    def blocks_of(matrix):
        return [matrix[:, at : at + D].reshape(owners, rows_of, D) for at in range(0, matrix.shape[1], D)]

    for depth in reversed(range(LAYERS)):
        gain_one, shift_one, query_shift, value_shift, out_shift, gain_two, shift_two, fall_shift = [
            vectors[depth, j] for j in range(8)
        ]
        mix_weight, out_weight = mix_weights[depth], out_weights[depth]
        rise_weight, fall_weight = feed[depth]
        (stream_in, normed, halo_normed, queries, pairs, halo_pairs, lse, attended, stream_mid, normed_two, before, hidden) = kept[depth]
        grad_fall = grad_stream.astype(BF16)
        fall_grad = dot_rows(hidden, grad_fall).astype(BF16)
        fall_shift_grad = column_sum(grad_fall)
        grad_before = (dot_back(grad_fall, fall_weight) * gelu_slope(before)).astype(BF16)
        rise_grad = dot_rows(normed_two, grad_before).astype(BF16)
        rise_shift_grad = column_sum(grad_before)
        grad_normed_two = dot_back(grad_before, rise_weight)
        norm_pair_two = jax.vjp(layer_norm, stream_mid, gain_two, shift_two)
        grad_mid_norm, gain_two_grad, shift_two_grad = norm_pair_two[1](grad_normed_two)
        grad_mid = grad_stream + grad_mid_norm
        grad_branch = grad_mid.astype(BF16)
        out_grad = dot_rows(attended, grad_branch).astype(BF16)
        out_shift_grad = column_sum(grad_branch)
        grad_attended = dot_back(grad_branch, out_weight).astype(BF16)
        if depth == 0 and by_hops:
            with jax.named_scope("feed_core"):
                feed_terms = reduce_core(rise_grad), reduce_core(fall_grad)
            feed_line = reduce_line(*feed_terms, "feed")
        with jax.named_scope(f"back{depth}"):
            dq, dpairs, dhalo = attend_back(segment, valid, queries, pairs, halo_pairs, grad_attended, lse, rise_grad)
        halo_back = swap_seq(dot_back(dhalo, mix_weight[:, D:]).astype(BF16)).astype(F32)
        normed_all = jnp.concatenate([normed, halo_normed], axis=0)
        dpairs_all = jnp.concatenate([dpairs, dhalo], axis=0)
        query_grad = dot_rows(normed, dq).astype(BF16)
        pair_grad = dot_rows(normed_all, dpairs_all).astype(BF16)
        if depth == 1:
            parts = [fall_grad.reshape(owners, -1, D)]
            for matrix in (rise_grad, out_grad, query_grad, pair_grad):
                parts += blocks_of(matrix)
            with jax.named_scope("scatter1"):
                high_sum = scattered(jnp.concatenate(parts, axis=1).reshape(-1, D))
        elif by_hops:
            with jax.named_scope("mix_core"):
                mix_terms = [reduce_core(matrix) for matrix in (pair_grad, query_grad, out_grad)]
            pair_terms = mix_terms[0]
            rest_terms = [jnp.concatenate([a, b], axis=-1) for a, b in zip(mix_terms[1], mix_terms[2])]
            mix_line = reduce_line(pair_terms, rest_terms, "mix")
        query_shift_grad = column_sum(dq)
        value_shift_grad = column_sum(dpairs_all).reshape(PAIRS, 2, PAIR)[:, 1].reshape(D)
        grad_normed = dot_back(dq, mix_weight[:, :D]) + dot_back(dpairs, mix_weight[:, D:])
        grad_normed = jnp.concatenate([grad_normed[:HALF] + halo_back, grad_normed[HALF:]], axis=0)
        norm_pair_one = jax.vjp(layer_norm, stream_in, gain_one, shift_one)
        grad_in_norm, gain_one_grad, shift_one_grad = norm_pair_one[1](grad_normed)
        grad_stream = grad_mid + grad_in_norm
        small_grads[depth] = jnp.concatenate(
            [
                member.reshape(owners, 1, rows_of)
                for member in (
                    gain_one_grad,
                    shift_one_grad,
                    query_shift_grad,
                    value_shift_grad,
                    out_shift_grad,
                    gain_two_grad,
                    shift_two_grad,
                    fall_shift_grad,
                )
            ]
            + [rise_shift_grad.reshape(owners, 4, rows_of)],
            axis=1,
        )

    small_all = jnp.concatenate(small_grads, axis=1).reshape(owners, -1)
    high_sum = over_seq(high_sum)

    def columns(block_rows, count):
        return block_rows.reshape(count, rows_of, D).swapaxes(0, 1).reshape(rows_of, count * D)

    at = [0, 4, 8, 9, 10, 12]
    fall_high, rise_high, out_high, query_high, pair_high = [
        high_sum[rows_of * low_row : rows_of * high_row] for low_row, high_row in zip(at[:-1], at[1:])
    ]
    rise_high, pair_high = columns(rise_high, 4), columns(pair_high, 2)
    if by_hops:
        rise_line, fall_line = feed_line
        mine = along_z(jnp.concatenate([rise_line, side_by_side(fall_line)], axis=-1), "feed")
        with jax.named_scope("feed_last"):
            other = swap_seq(mine)
        rise_low = both_halves(mine, other, 0, FF // 2)
        fall_low = jnp.concatenate(
            [both_halves(mine, other, FF // 2 + j * D // 2, D // 2) for j in range(4)], axis=0
        )
        with jax.named_scope("small"):
            small_all = small_all + hop_core(small_all)
            small_all = small_all + hop_y(small_all)
            small_all = small_all + swap_seq(small_all)
        me = lax.axis_index("fsdp")
        small_line = pick(small_all.reshape(4, 4, -1), me % 4, 1).astype(BF16).reshape(4, rows_of, -1)
        width = small_line.shape[-1]
        small_line = jnp.pad(small_line, ((0, 0), (0, 0), (0, 128 - width)))
        mine = along_z(jnp.concatenate([*mix_line, small_line], axis=-1), "mix")
        with jax.named_scope("mix_last"):
            other = swap_seq(mine[:, : 2 * D])
        pair_low = both_halves(mine, other, 0, D)
        rest_low = both_halves(mine, other, D, D)
        query_low, out_low = rest_low[:, :D], rest_low[:, D:]
        small_sum = mine[:, 2 * D : 2 * D + width].astype(F32).reshape(LAYERS, 12, rows_of)
    else:
        fall_low, rise_low, out_low, query_low, pair_low = [
            over_seq(scattered(matrix)) for matrix in (fall_grad, rise_grad, out_grad, query_grad, pair_grad)
        ]
        small_sum = over_seq(scattered(small_all.astype(BF16))).reshape(LAYERS, 12, rows_of)

    def mix_out(query, pair):
        return jnp.concatenate([query, unpair_columns(pair)], axis=1)

    layer_output = near_first(stream.astype(BF16))[None]
    input_grad = near_first(grad_stream)[None]
    return (
        layer_output,
        input_grad,
        small_sum[:, 0],
        small_sum[:, 1],
        jnp.stack([mix_out(query_low, pair_low), mix_out(query_high, pair_high)]),
        small_sum[:, 2],
        small_sum[:, 3],
        jnp.stack([out_low, out_high]),
        small_sum[:, 4],
        small_sum[:, 5],
        small_sum[:, 6],
        jnp.stack([rise_low, rise_high]),
        small_sum[:, 8:].reshape(LAYERS, 4 * rows_of),
        jnp.stack([fall_low, fall_high]),
        small_sum[:, 7],
    )


def solution(mesh):
    vector, matrix = P(None, "fsdp"), P(None, "fsdp", None)
    tokens, places = P("fsdp", "seq", None), P("fsdp", None)
    return jax.shard_map(
        local,
        mesh=mesh,
        in_specs=(
            tokens,
            places,
            places,
            vector,
            vector,
            matrix,
            vector,
            vector,
            matrix,
            vector,
            vector,
            vector,
            matrix,
            vector,
            matrix,
            vector,
            tokens,
        ),
        out_specs=(
            tokens,
            tokens,
            vector,
            vector,
            matrix,
            vector,
            vector,
            matrix,
            vector,
            vector,
            vector,
            matrix,
            vector,
            matrix,
            vector,
        ),
        check_vma=False,
    )
```

```python
import jax
import jax.numpy as jnp
from jax import lax
from jax.experimental import pallas as pl
from jax.experimental.pallas import tpu as pltpu
from jax.sharding import PartitionSpec as P


D = 768
HD = 64
FF = 3072
LAYERS = 2
PAIR = 128
PAIRS = D // PAIR
HALF = 256

EPS = 1e-06
NEG = -1e30
F32 = jnp.float32
BF16 = jnp.bfloat16


def layer_norm(values, norm_gain, norm_shift):
    center = values - jnp.mean(values, axis=-1, keepdims=True)
    spread = jnp.mean(center * center, axis=-1, keepdims=True)
    return center * lax.rsqrt(spread + EPS) * norm_gain + norm_shift


def gelu_exact(values):
    return 0.5 * values * (1.0 + lax.erf(values * 2.0 ** (-0.5)))


def gelu_slope(values):
    return 0.5 * (1.0 + lax.erf(values * 2.0 ** (-0.5))) + values * (
        jnp.exp(-0.5 * values * values) * (2.0 * jnp.pi) ** (-0.5)
    )


def dot(left_side, right_side):
    return jnp.dot(left_side, right_side, preferred_element_type=F32)


def dot_rows(left_side, right_side):
    return lax.dot_general(left_side, right_side, (((0,), (0,)), ((), ())), preferred_element_type=F32)


def dot_back(left_side, right_side):
    return lax.dot_general(left_side, right_side, (((1,), (1,)), ((), ())), preferred_element_type=F32)


def column_sum(values):
    return dot(jnp.ones((8, values.shape[0]), BF16), values)[0]


def attend_kernel(seg_row, seg_col, valid_col, q_ref, kv_ref, halo_ref, out_ref, lse_ref, bias):
    @pl.when(pl.program_id(0) == 0)
    def _():
        rows = lax.broadcasted_iota(jnp.int32, bias.shape, 0)
        columns = lax.broadcasted_iota(jnp.int32, bias.shape, 1)
        allowed = (seg_col[...] == seg_row[...]) & ((valid_col[...] == 1) | (rows == columns))
        bias[...] = jnp.where(allowed, 0.0, NEG)

    lane = lax.broadcasted_iota(jnp.int32, (HALF, PAIR), 1)
    keys, halo_keys = kv_ref[:, :PAIR], halo_ref[:, :PAIR]
    values_t, halo_values_t = kv_ref[:, PAIR:].T, halo_ref[:, PAIR:].T
    units = [(block, head) for block in range(2) for head in range(2)]

    def scores_of(block, head):
        rows = slice(block * HALF, (block + 1) * HALF)
        queries = q_ref[rows, :] * jnp.asarray(HD ** (-0.5), BF16)
        query = jnp.where((lane // HD) == head, queries, jnp.zeros_like(queries))
        found = [dot_back(keys, query) + bias[: 2 * HALF, rows]]
        if block == 0:
            found.append(dot_back(halo_keys, query) + bias[2 * HALF :, rows])
        return found

    parts, coming = [], scores_of(*units[0])
    for place, (block, head) in enumerate(units):
        rows, dims = slice(block * HALF, (block + 1) * HALF), slice(head * HD, (head + 1) * HD)
        scores = coming
        if place + 1 < len(units):
            coming = scores_of(*units[place + 1])
        top = jnp.max(scores[0], axis=0, keepdims=True)
        for more in scores[1:]:
            top = jnp.maximum(top, jnp.max(more, axis=0, keepdims=True))
        terms = [jnp.exp(part - top) for part in scores]
        total = sum(jnp.sum(part, axis=0, keepdims=True) for part in terms)
        found = sum(dot(side[dims, :], part.astype(BF16)) for side, part in zip((values_t, halo_values_t), terms))
        parts.append(found * (1.0 / total))
        lse_ref[0, head : head + 1, rows] = top + jnp.log(total)
        if head == 1:
            out_ref[rows, :] = jnp.concatenate(parts, axis=0).T.astype(BF16)
            parts = []


def attend(segment, valid, queries, pairs, halo_pairs):
    rows, reach = queries.shape[0], segment.shape[0]
    whole = lambda shape: pl.BlockSpec(shape, lambda i: (0, 0))
    return pl.pallas_call(
        attend_kernel,
        grid=(PAIRS,),
        in_specs=[
            whole((1, rows)),
            whole((reach, 1)),
            whole((reach, 1)),
            pl.BlockSpec((rows, PAIR), lambda i: (0, i)),
            pl.BlockSpec((rows, 2 * PAIR), lambda i: (0, i)),
            pl.BlockSpec((HALF, 2 * PAIR), lambda i: (0, i)),
        ],
        out_specs=[
            pl.BlockSpec((rows, PAIR), lambda i: (0, i)),
            pl.BlockSpec((1, 2, rows), lambda i: (i, 0, 0)),
        ],
        out_shape=[
            jax.ShapeDtypeStruct((rows, D), BF16),
            jax.ShapeDtypeStruct((PAIRS, 2, rows), F32),
        ],
        scratch_shapes=[pltpu.VMEM((reach, rows), F32)],
        cost_estimate=pl.CostEstimate(flops=4 * 5 * 65536 * D, bytes_accessed=6 << 20, transcendentals=5 * 65536 * 12),
        name="attend",
    )(segment[None, :rows], segment[:, None], valid[:, None], queries, pairs, halo_pairs)


def attend_back_kernel(
    seg_row, seg_col, valid_col, q_ref, kv_ref, halo_ref, grad_ref, lse_ref, _, dq_ref, dkv_ref, dhalo_ref, bias
):
    @pl.when(pl.program_id(0) == 0)
    def _():
        rows = lax.broadcasted_iota(jnp.int32, bias.shape, 0)
        columns = lax.broadcasted_iota(jnp.int32, bias.shape, 1)
        allowed = (seg_col[...] == seg_row[...]) & ((valid_col[...] == 1) | (rows == columns))
        bias[...] = jnp.where(allowed, 0.0, NEG)

    lane = lax.broadcasted_iota(jnp.int32, (HALF, PAIR), 1)
    keys, values = kv_ref[:, :PAIR], kv_ref[:, PAIR:]
    halo_keys, halo_values = halo_ref[:, :PAIR], halo_ref[:, PAIR:]
    keys_t, halo_keys_t = keys.T, halo_keys.T
    scale = jnp.asarray(HD ** (-0.5), BF16)
    plus = lambda total, term: term if total is None else total + term
    units = [(block, head) for block in range(2) for head in range(2)]

    def start(block, head):
        rows = slice(block * HALF, (block + 1) * HALF)
        mine = (lane // HD) == head
        query = jnp.where(mine, q_ref[rows, :] * scale, jnp.zeros((HALF, PAIR), BF16))
        grad = jnp.where(mine, grad_ref[rows, :], jnp.zeros((HALF, PAIR), BF16))
        sides = [(keys, values, slice(0, 2 * HALF))]
        if block == 0:
            sides.append((halo_keys, halo_values, slice(2 * HALF, 3 * HALF)))
        return query, grad, [(dot_back(k, query) + bias[at, rows], dot_back(v, grad)) for k, v, at in sides]

    sums, dq_parts, coming = [None] * 4, [], start(*units[0])
    for place, (block, head) in enumerate(units):
        rows, dims = slice(block * HALF, (block + 1) * HALF), slice(head * HD, (head + 1) * HD)
        query, grad, sides = coming
        if place + 1 < len(units):
            coming = start(*units[place + 1])
        lse = lse_ref[0, head : head + 1, rows]
        chances = [jnp.exp(scores - lse) for scores, _ in sides]
        inner = sum(jnp.sum(c * back, axis=0, keepdims=True) for c, (_, back) in zip(chances, sides))
        dq = None
        for side, (chance, (_, back)) in enumerate(zip(chances, sides)):
            slopes = (chance * (back - inner)).astype(BF16)
            dq = plus(dq, dot((keys_t, halo_keys_t)[side][dims, :], slopes))
            sums[2 * side] = plus(sums[2 * side], dot(slopes, query))
            sums[2 * side + 1] = plus(sums[2 * side + 1], dot(chance.astype(BF16), grad))
        dq_parts.append(dq)
        if head == 1:
            dq_ref[rows, :] = (jnp.concatenate(dq_parts, axis=0).T * HD ** (-0.5)).astype(BF16)
            dq_parts = []
    dk, dv, dk_halo, dv_halo = sums
    dkv_ref[:, :PAIR] = dk.astype(BF16)
    dkv_ref[:, PAIR:] = dv.astype(BF16)
    dhalo_ref[:, :PAIR] = dk_halo.astype(BF16)
    dhalo_ref[:, PAIR:] = dv_halo.astype(BF16)


def attend_back(segment, valid, queries, pairs, halo_pairs, grads, lse, earlier):
    rows, reach = queries.shape[0], segment.shape[0]
    whole = lambda shape: pl.BlockSpec(shape, lambda i: (0, 0))
    tokens = pl.BlockSpec((rows, PAIR), lambda i: (0, i))
    both = pl.BlockSpec((rows, 2 * PAIR), lambda i: (0, i))
    halo = pl.BlockSpec((HALF, 2 * PAIR), lambda i: (0, i))
    return pl.pallas_call(
        attend_back_kernel,
        grid=(PAIRS,),
        in_specs=[
            whole((1, rows)),
            whole((reach, 1)),
            whole((reach, 1)),
            tokens,
            both,
            halo,
            tokens,
            pl.BlockSpec((1, 2, rows), lambda i: (i, 0, 0)),
            pl.BlockSpec(memory_space=pl.ANY),
        ],
        out_specs=[tokens, both, halo],
        out_shape=[
            jax.ShapeDtypeStruct((rows, D), BF16),
            jax.ShapeDtypeStruct((rows, 2 * D), BF16),
            jax.ShapeDtypeStruct((HALF, 2 * D), BF16),
        ],
        scratch_shapes=[pltpu.VMEM((reach, rows), F32)],
        cost_estimate=pl.CostEstimate(flops=10 * 5 * 65536 * D, bytes_accessed=10 << 20, transcendentals=5 * 65536 * 12),
        name="attend_back",
    )(segment[None, :rows], segment[:, None], valid[:, None], queries, pairs, halo_pairs, grads, lse, earlier)


def swap_seq(values):
    return lax.ppermute(values, "seq", [(0, 1), (1, 0)])


def pair_columns(matrix):
    return matrix.reshape(-1, 2, PAIRS, PAIR).swapaxes(1, 2).reshape(-1, 2 * D)


def unpair_columns(matrix):
    return matrix.reshape(-1, PAIRS, 2, PAIR).swapaxes(1, 2).reshape(-1, 2 * D)


HOPS = 16
SMALL = 128


def place(z, y, core):
    return (z * 2 + y) * 2 + core


def hop(values, target):
    pairs = []
    for z in range(4):
        for y in range(2):
            for core in range(2):
                goal = target(z, y, core)
                if goal is not None:
                    pairs.append((place(z, y, core), place(*goal)))
    return lax.ppermute(values, "fsdp", pairs)


def hop_core(values):
    return hop(values, lambda z, y, core: (z, y, 1 - core))


def hop_y(values):
    return hop(values, lambda z, y, core: (z, 1 - y, core))


def up(values, sources=(0, 1, 2)):
    return hop(values, lambda z, y, core: (z + 1, y, core) if z in sources else None)


def down(values, sources=(1, 2, 3)):
    return hop(values, lambda z, y, core: (z - 1, y, core) if z in sources else None)


def pick(values, index, axis):
    return lax.dynamic_index_in_dim(values, index, axis, keepdims=False)


def half_of(values, x):
    half = values.shape[-1] // 2
    return lax.dynamic_slice_in_dim(values, x * half, half, axis=values.ndim - 1)


def side_by_side(blocks):
    rows = D // HOPS
    count = blocks.shape[-2] // rows
    return jnp.concatenate([blocks[..., j * rows : (j + 1) * rows, :] for j in range(count)], axis=-1)


def gather_hops(rise_shard, fall_shard):
    x = lax.axis_index("seq")
    mine = jnp.concatenate([half_of(rise_shard, x), side_by_side(half_of(fall_shard, x))], axis=1)
    up_one = up(mine)
    down_one = down(mine)
    up_two = up(up_one, (1, 2))
    down_two = down(down_one, (1, 2))
    up_three = up(up_two, (2,))
    down_three = down(down_two, (1,))
    line = jnp.stack([mine, down_one + up_three, down_two + up_two, down_three + up_one])
    split = mine.shape[1] // 2
    line_a, line_b = line[:, :, :split], line[:, :, split:]
    first_a = jnp.concatenate([line_a, hop_y(line_a)], axis=0)
    first_b = jnp.concatenate([line_b, swap_seq(line_b)], axis=0)
    second_a = swap_seq(first_a)
    second_b = hop_y(first_b)
    third_a = hop_core(first_a)
    third_b = hop_core(first_b)
    fourth_a = hop_core(second_a)
    fourth_b = hop_core(second_b)
    return [first_a, second_a, third_a, fourth_a, first_b, second_b, third_b, fourth_b]


def along_z(line):
    z = lax.axis_index("fsdp") // 4
    rising = falling = None
    for step in (3, 2, 1):
        low, high = pick(line, jnp.minimum(z + step, 3), 0), pick(line, jnp.maximum(z - step, 0), 0)
        rising = up(low if rising is None else low + rising, tuple(range(4 - step)))
        falling = down(high if falling is None else high + falling, tuple(range(step, 4)))
    return (pick(line, z, 0).astype(F32) + rising.astype(F32) + falling.astype(F32)).astype(BF16)


def reduce_core(matrix):
    core = lax.axis_index("fsdp") % 2
    both = matrix.reshape(8, 2, -1, matrix.shape[-1])
    return [pick(both, core, 1), hop_core(pick(both, 1 - core, 1))]


def total(terms):
    result = terms[0].astype(F32)
    for term in terms[1:]:
        result = result + term.astype(F32)
    return result.astype(BF16)


def sent_x(terms):
    x = lax.axis_index("seq")
    return [half_of(term, x) for term in terms] + [swap_seq(total([half_of(term, 1 - x) for term in terms]))]


def sent_y(terms):
    y = (lax.axis_index("fsdp") // 2) % 2
    terms = [term.reshape((4, 2) + term.shape[1:]) for term in terms]
    return [pick(term, y, 1) for term in terms] + [hop_y(total([pick(term, 1 - y, 1) for term in terms]))]


def reduce_line(first_x, first_y):
    if first_x is not None:
        first_x = sent_x(first_x)
    first_y = sent_y(first_y)
    if first_x is not None:
        first_x = total(sent_y(first_x))
    first_y = total(sent_x(first_y))
    return first_x, first_y


def both_halves(mine, other, start, size):
    here, there = mine[:, start : start + size], other[:, start : start + size]
    left = lax.axis_index("seq") == 0
    return jnp.concatenate([jnp.where(left, here, there), jnp.where(left, there, here)], axis=1).astype(F32)


def assemble_kernel(*refs):
    sources, (rise, fall, held_rise, held_fall, in_sems, out_sems) = refs[:8], refs[-6:]
    my_x, me = lax.axis_index("seq"), lax.axis_index("fsdp")
    my_core, my_y, my_z = me % 2, (me // 2) % 2, me // 4
    z_of = [(my_z + slot) % 4 for slot in range(4)]
    rows = D // HOPS
    for index, source in enumerate(sources):
        is_rise, other_core, second = index < 4, (index % 4) // 2, index % 2
        core = (my_core + other_core) % 2
        for slot in range(8):
            turn, z = slot // 4, z_of[slot % 4]
            x = (my_x + (second if is_rise else turn)) % 2
            y = (my_y + (turn if is_rise else second)) % 2
            owner = (z * 2 + y) * 2 + core
            if is_rise:
                pltpu.make_async_copy(
                    source.at[slot],
                    held_rise.at[
                        pl.ds(pl.multiple_of(owner * rows, 16), rows),
                        pl.ds(pl.multiple_of(x * (FF // 2), 128), FF // 2),
                    ],
                    in_sems.at[0],
                ).start()
                continue
            for block in range(4):
                pltpu.make_async_copy(
                    source.at[slot, :, pl.ds(block * (D // 2), D // 2)],
                    held_fall.at[
                        pl.ds(pl.multiple_of((owner * 4 + block) * rows, 16), rows),
                        pl.ds(pl.multiple_of(x * (D // 2), 128), D // 2),
                    ],
                    in_sems.at[1],
                ).start()
    for which, (held, out) in enumerate(((held_rise, rise), (held_fall, fall))):
        pltpu.make_async_copy(held, held, in_sems.at[which]).wait()
        pltpu.make_async_copy(held, out, out_sems.at[which]).start()
    for which, (held, out) in enumerate(((held_rise, rise), (held_fall, fall))):
        pltpu.make_async_copy(held, out, out_sems.at[which]).wait()


def assemble(buffers, earlier):
    shapes = [(D, FF), (FF, D)]
    return pl.pallas_call(
        assemble_kernel,
        in_specs=[pl.BlockSpec(memory_space=pl.ANY)] * 9,
        out_specs=[pl.BlockSpec(memory_space=pl.ANY)] * 2,
        out_shape=[jax.ShapeDtypeStruct(shape, BF16) for shape in shapes],
        scratch_shapes=[pltpu.VMEM(shape, BF16) for shape in shapes]
        + [pltpu.SemaphoreType.DMA((2,)), pltpu.SemaphoreType.DMA((2,))],
        compiler_params=pltpu.CompilerParams(vmem_limit_bytes=24 << 20),
        cost_estimate=pl.CostEstimate(flops=0, bytes_accessed=4 * 2 * D * FF, transcendentals=0),
        name="assemble",
    )(*buffers, earlier)


def local(
    layer_input,
    segment_ids,
    key_valid,
    first_gain,
    first_shift,
    input_weight,
    query_bias,
    value_bias,
    output_weight,
    output_bias,
    second_gain,
    second_shift,
    up_weight,
    up_bias,
    down_weight,
    down_bias,
    output_cotangent,
):
    right = lax.axis_index("seq") == 1
    rows_of = input_weight.shape[1]
    owners = D // rows_of

    def near_first(values):
        turned = jnp.concatenate([values[HALF:], values[:HALF]], axis=0)
        return jnp.where(right, values, turned)

    def by_block(values):
        blocks = values.reshape(4, HALF)
        return jnp.where(
            right,
            jnp.concatenate([blocks[2], blocks[3], blocks[1]]),
            jnp.concatenate([blocks[1], blocks[0], blocks[2]]),
        )

    def gather(shard):
        return lax.all_gather(shard, "fsdp", axis=0, tiled=False)

    segment, valid = by_block(segment_ids[0]), by_block(key_valid[0])

    smalls = [first_gain, first_shift, query_bias, value_bias, output_bias, second_gain, second_shift, down_bias]
    small = jnp.concatenate([member.reshape(-1) for member in smalls] + [up_bias.reshape(-1)])
    vector_side = 8 * LAYERS * rows_of
    side = rows_of * 128
    small_block = jnp.pad(small, (0, side - small.shape[0])).reshape(rows_of, 128)

    def mixing(depth):
        return [input_weight[depth][:, :D], pair_columns(input_weight[depth][:, D:])]

    low = gather(jnp.concatenate(mixing(0) + [small_block], axis=1)).reshape(D, -1)
    high = gather(jnp.concatenate(mixing(1) + [output_weight[0], output_weight[1]], axis=1)).reshape(D, -1)
    mix_weights = [low[:, : 3 * D], high[:, : 3 * D]]
    out_weights = [high[:, 3 * D : 4 * D], high[:, 4 * D :]]
    smalls_full = low[:, 3 * D :].reshape(owners, side)[:, : small.shape[0]].astype(F32)
    vectors = smalls_full[:, :vector_side].reshape(owners, -1, rows_of).swapaxes(0, 1).reshape(8, LAYERS, D)
    up_biases = smalls_full[:, vector_side:].reshape(owners, LAYERS, -1).swapaxes(0, 1).reshape(LAYERS, FF)
    by_hops = owners == HOPS
    if by_hops:
        pieces = [gather_hops(up_weight[depth], down_weight[depth]) for depth in range(LAYERS)]

    def feed_weights(depth, earlier):
        if by_hops:
            return assemble(pieces[depth], earlier)
        return gather(up_weight[depth]).reshape(D, FF), gather(down_weight[depth]).reshape(FF, D)

    stream = near_first(layer_input[0]).astype(F32)
    kept, feed = [], []
    for depth in range(LAYERS):
        gain_one, shift_one, query_shift, value_shift, out_shift, gain_two, shift_two, fall_shift = [
            vectors[j, depth] for j in range(8)
        ]
        mix_weight, out_weight = mix_weights[depth], out_weights[depth]
        normed = layer_norm(stream, gain_one, shift_one).astype(BF16)
        halo_normed = swap_seq(normed[:HALF])
        pair_shift = jnp.stack([jnp.zeros((PAIRS, PAIR), F32), value_shift.reshape(PAIRS, PAIR)], axis=1).reshape(-1)
        queries = (dot(normed, mix_weight[:, :D]) + query_shift).astype(BF16)
        pairs = (dot(normed, mix_weight[:, D:]) + pair_shift).astype(BF16)
        halo_pairs = (dot(halo_normed, mix_weight[:, D:]) + pair_shift).astype(BF16)
        attended, lse = attend(segment, valid, queries, pairs, halo_pairs)
        stream_mid = stream + (dot(attended, out_weight) + out_shift)
        normed_two = layer_norm(stream_mid, gain_two, shift_two).astype(BF16)
        rise_weight, fall_weight = feed_weights(depth, attended)
        feed.append((rise_weight, fall_weight))
        before = dot(normed_two, rise_weight) + up_biases[depth]
        hidden = gelu_exact(before).astype(BF16)
        stream_next = stream_mid + (dot(hidden, fall_weight) + fall_shift)
        kept.append((stream, normed, halo_normed, queries, pairs, halo_pairs, lse, attended, stream_mid, normed_two, before, hidden))
        stream = stream_next

    grad_stream = near_first(output_cotangent[0]).astype(F32)
    small_grads, feed_sums, mix_sums = [None] * LAYERS, [None] * LAYERS, [None] * LAYERS

    def scattered(matrix):
        return lax.psum_scatter(matrix, "fsdp", scatter_dimension=0, tiled=True)

    def over_seq(mine):
        return mine.astype(F32) + swap_seq(mine).astype(F32)

    def small_matrix():
        rows = jnp.stack([small_grads[layer][0][j] for j in range(8) for layer in range(LAYERS)])
        rises = jnp.stack([small_grads[layer][1] for layer in range(LAYERS)])
        return jnp.concatenate(
            [
                rows.reshape(-1, owners, rows_of).swapaxes(0, 1).reshape(owners, -1),
                rises.reshape(LAYERS, owners, -1).swapaxes(0, 1).reshape(owners, -1),
            ],
            axis=1,
        )

    def blocks_of(matrix):
        return [matrix[:, at : at + D].reshape(owners, rows_of, D) for at in range(0, matrix.shape[1], D)]

    for depth in reversed(range(LAYERS)):
        gain_one, shift_one, query_shift, value_shift, out_shift, gain_two, shift_two, fall_shift = [
            vectors[j, depth] for j in range(8)
        ]
        mix_weight, out_weight = mix_weights[depth], out_weights[depth]
        rise_weight, fall_weight = feed[depth]
        (stream_in, normed, halo_normed, queries, pairs, halo_pairs, lse, attended, stream_mid, normed_two, before, hidden) = kept[depth]
        grad_fall = grad_stream.astype(BF16)
        fall_grad = dot_rows(hidden, grad_fall).astype(BF16)
        fall_shift_grad = column_sum(grad_fall)
        grad_before = (dot_back(grad_fall, fall_weight) * gelu_slope(before)).astype(BF16)
        rise_grad = dot_rows(normed_two, grad_before).astype(BF16)
        rise_shift_grad = column_sum(grad_before)
        if depth == 0 and by_hops:
            feed_packed = rise_grad
            fall_terms = reduce_core(fall_grad)
            _, fall_line = reduce_line(None, fall_terms)
        else:
            feed_packed = jnp.concatenate([fall_grad.reshape(owners, -1, D)] + blocks_of(rise_grad), axis=1)
            feed_packed = feed_packed.reshape(-1, D)
        feed_sums[depth] = scattered(feed_packed)
        grad_normed_two = dot_back(grad_before, rise_weight)
        norm_pair_two = jax.vjp(layer_norm, stream_mid, gain_two, shift_two)
        grad_mid_norm, gain_two_grad, shift_two_grad = norm_pair_two[1](grad_normed_two)
        grad_mid = grad_stream + grad_mid_norm
        grad_branch = grad_mid.astype(BF16)
        out_grad = dot_rows(attended, grad_branch).astype(BF16)
        out_shift_grad = column_sum(grad_branch)
        grad_attended = dot_back(grad_branch, out_weight).astype(BF16)
        if by_hops:
            out_terms = reduce_core(out_grad)
        dq, dpairs, dhalo = attend_back(segment, valid, queries, pairs, halo_pairs, grad_attended, lse, feed_packed)
        halo_back = dot_back(dhalo, mix_weight[:, D:]).astype(BF16)
        halo_back = swap_seq(halo_back).astype(F32)
        normed_all = jnp.concatenate([normed, halo_normed], axis=0)
        dpairs_all = jnp.concatenate([dpairs, dhalo], axis=0)
        query_grad = dot_rows(normed, dq).astype(BF16)
        pair_grad = dot_rows(normed_all, dpairs_all).astype(BF16)
        query_shift_grad = column_sum(dq)
        value_shift_grad = column_sum(dpairs_all).reshape(PAIRS, 2, PAIR)[:, 1].reshape(D)
        if by_hops:
            pair_terms, query_terms = reduce_core(pair_grad), reduce_core(query_grad)
        grad_normed = dot_back(dq, mix_weight[:, :D]) + dot_back(dpairs, mix_weight[:, D:])
        grad_normed = jnp.concatenate([grad_normed[:HALF] + halo_back, grad_normed[HALF:]], axis=0)
        norm_pair_one = jax.vjp(layer_norm, stream_in, gain_one, shift_one)
        grad_in_norm, gain_one_grad, shift_one_grad = norm_pair_one[1](grad_normed)
        grad_stream = grad_mid + grad_in_norm
        small_grads[depth] = (
            [
                gain_one_grad,
                shift_one_grad,
                query_shift_grad,
                value_shift_grad,
                out_shift_grad,
                gain_two_grad,
                shift_two_grad,
                fall_shift_grad,
            ],
            rise_shift_grad,
        )
        if not by_hops:
            mix_sums[depth] = [over_seq(scattered(matrix)) for matrix in (pair_grad, query_grad, out_grad)]
            continue
        rest_terms = [jnp.concatenate(members, axis=-1) for members in zip(query_terms, out_terms)]
        mix_sums[depth] = reduce_line(pair_terms, rest_terms)

    def columns(block_rows, count):
        return block_rows.reshape(count, rows_of, D).swapaxes(0, 1).reshape(rows_of, count * D)

    for depth in reversed(range(LAYERS)):
        feed_sums[depth] = over_seq(feed_sums[depth])
    fall_high, rise_high = feed_sums[1][: 4 * rows_of], columns(feed_sums[1][4 * rows_of :], 4)

    if by_hops:
        rise_low = feed_sums[0]
        small = small_matrix()
        small = small + hop_core(small)
        small = small + swap_seq(small)
        small = small + hop_y(small)
        small = pick(small.reshape(4, 4, -1), lax.axis_index("fsdp") % 4, 1).astype(BF16).reshape(4, rows_of, -1)
        small_width = small.shape[-1]
        small = jnp.pad(small, ((0, 0), (0, 0), (0, SMALL - small_width)))
        line = jnp.concatenate([*mix_sums[1], side_by_side(fall_line), *mix_sums[0], small], axis=-1)
        mine = along_z(line)
        other = swap_seq(mine[:, : 6 * D])
        fall_low = jnp.concatenate(
            [both_halves(mine, other, 2 * D + j * D // 2, D // 2) for j in range(4)], axis=0
        )
        for depth in range(LAYERS):
            start = 0 if depth == 1 else 4 * D
            pair, rest = both_halves(mine, other, start, D), both_halves(mine, other, start + D, D)
            mix_sums[depth] = pair, rest[:, :D], rest[:, D:]
        small_sum = mine[:, 6 * D : 6 * D + small_width].astype(F32).reshape(-1)
    else:
        fall_low, rise_low = feed_sums[0][: 4 * rows_of], columns(feed_sums[0][4 * rows_of :], 4)
        small_sum = over_seq(scattered(small_matrix().astype(BF16))).reshape(-1)
    rise_shifts = small_sum[vector_side:].reshape(LAYERS, -1)
    small_sum = small_sum[:vector_side].reshape(8, LAYERS, rows_of)

    def mix_out(query, pair):
        return jnp.concatenate([query, unpair_columns(pair)], axis=1)

    layer_output = near_first(stream.astype(BF16))[None]
    input_grad = near_first(grad_stream)[None]
    return (
        layer_output,
        input_grad,
        small_sum[0],
        small_sum[1],
        jnp.stack([mix_out(query, pair) for pair, query, _ in mix_sums]),
        small_sum[2],
        small_sum[3],
        jnp.stack([out for _, _, out in mix_sums]),
        small_sum[4],
        small_sum[5],
        small_sum[6],
        jnp.stack([rise_low, rise_high]),
        rise_shifts,
        jnp.stack([fall_low, fall_high]),
        small_sum[7],
    )


def solution(mesh):
    vector, matrix = P(None, "fsdp"), P(None, "fsdp", None)
    tokens, places = P("fsdp", "seq", None), P("fsdp", None)
    return jax.shard_map(
        local,
        mesh=mesh,
        in_specs=(
            tokens,
            places,
            places,
            vector,
            vector,
            matrix,
            vector,
            vector,
            matrix,
            vector,
            vector,
            vector,
            matrix,
            vector,
            matrix,
            vector,
            tokens,
        ),
        out_specs=(
            tokens,
            tokens,
            vector,
            vector,
            matrix,
            vector,
            vector,
            matrix,
            vector,
            vector,
            vector,
            matrix,
            vector,
            matrix,
            vector,
        ),
        check_vma=False,
    )
```
